32 devices in a mesh: lat: 4 (over z), lon: 8 (over y, x, core).
Axes of the slice: x: 2, y: 2, z: 4, core: 2. Of those that a mesh axis runs over, the one named last changes fastest.
Arguments:
- inputs: bfloat16 [128, 360, 512], P('lat', 'lon'), may hold values from -6 to 6
- metric: float32 [128, 360], P('lat', 'lon'), may hold values from 0.5 to 2
- kernel_one: float32 [9, 512], replicated, may hold values from -2 to 2
- kernel_two: float32 [9, 512], replicated, may hold values from -2 to 2
- widths: int32 [128], P('lat'), may hold values from 0 to 90, as said below
- zonal_gains: bfloat16 [128, 181], P('lat'), may hold values from -0.19921875 to 0.19921875
- norm_gain: float32 [512], replicated, may hold values from 0.5 to 1.5
- weight_in: bfloat16 [512, 1024], replicated, may hold values from -0.25 to 0.25
- weight_out: bfloat16 [1024, 512], replicated, may hold values from -0.1875 to 0.1875
Outputs:
- updated: bfloat16 [128, 360, 512], P('lat', 'lon')
The draws below stay inside these ranges and needn't reach their ends.
Inputs may be any that keep to these rules, and one draw needn't show every extreme that they name: widths gives the zonal filter half-width of each latitude row.
All inputs are finite; a program needn't handle non-finite values.
Results may differ from the reference program's by a relative error of at most 0.0061.
Values may be sent and summed in bfloat16 or wider, within the bound.
A program may use at most 64 MiB of HBM per device.

```python
import math
import jax
import jax.numpy as jnp
from jax import lax

C = 512
HID = 1024
NLAT = 128
NLON = 360
BMAX = 90


def draw_widths(key, part):
    row_ids = jnp.arange(NLAT, dtype=jnp.int32)
    distance = jnp.minimum(row_ids, NLAT - 1 - row_ids)
    quarter = NLAT // 4
    base_width = BMAX - distance * BMAX // quarter
    jitter = jax.random.randint(key, (NLAT,), -(BMAX // 8), BMAX // 8 + 1, dtype=jnp.int32)
    result = jnp.clip(base_width + jitter, 0, BMAX)
    result = jnp.where(distance >= quarter, 0, result)
    result = jnp.where(distance == 0, BMAX, result)
    return result.astype(jnp.int32)


def block_scale(rng, shape, cuts, smallest, top_value):
    level = 1.0
    for axis_at, parts in cuts:
        steps = jax.random.uniform(jax.random.fold_in(jax.random.fold_in(rng, 6), axis_at), (parts,), jnp.float32, smallest / len(cuts), top_value / len(cuts))
        level = level * jnp.repeat(jnp.exp(steps), shape[axis_at] // parts).reshape((-1,) + (1,) * (len(shape) - 1 - axis_at))
    return level


def bell_draw(own_key, dims, spread, reach, shards=(), kind=jnp.bfloat16):
    drawn = spread * jax.random.normal(own_key, dims, jnp.float32)
    if shards:
        drawn = drawn * block_scale(own_key, dims, shards, -0.22, 0.18)
    return jnp.clip(drawn, -reach, reach).astype(kind)


def setup_inputs(seed: int = 0) -> dict:
    streams_of = jax.random.split(jax.random.key(seed), 10)
    return {
        "inputs": bell_draw(streams_of[0], (NLAT, NLON, C), 1.0, 6.0, ((0, 4), (1, 8))),
        "metric": jnp.clip(jnp.exp(math.log(2.0) - 1.3862944 * jax.random.uniform(streams_of[1], (NLAT, NLON), jnp.float32) ** block_scale(streams_of[1], (NLAT, NLON), ((0, 4), (1, 8)), -0.2, 0.2)), 0.5, 2.0),
        "kernel_one": bell_draw(streams_of[2], (9, C), 0.35, 2.0, (), jnp.float32),
        "kernel_two": bell_draw(streams_of[3], (9, C), 0.35, 2.0, (), jnp.float32),
        "widths": draw_widths(jax.random.fold_in(streams_of[9], 71), 0),
        "zonal_gains": bell_draw(streams_of[5], (NLAT, 2 * BMAX + 1), 0.04, 0.19921875, ((0, 4),)),
        "norm_gain": jnp.clip(1.0 + 0.1 * jax.random.normal(streams_of[6], (C,), jnp.float32), 0.5, 1.5),
        "weight_in": bell_draw(streams_of[7], (C, HID), C ** -0.5, 0.25),
        "weight_out": bell_draw(streams_of[8], (HID, C), HID ** -0.5, 0.1875),
    }


def gelu_tanh(values):
    return jax.nn.gelu(values, approximate=True)

def extend_whole(field):
    half = field.shape[1] // 2
    top_row = jnp.roll(field[:1], half, axis=1)
    bottom_row = jnp.roll(field[-1:], half, axis=1)
    tall = jnp.concatenate([top_row, field, bottom_row], axis=0)
    return jnp.concatenate([tall[:, -1:], tall, tall[:, :1]], axis=1)

def stencil(extended, kernel):
    height = extended.shape[0] - 2
    breadth = extended.shape[1] - 2
    summed = jnp.zeros((height, breadth, extended.shape[2]), jnp.float32)
    for tap in range(9):
        row_shift = tap // 3
        col_shift = tap % 3
        piece = extended[row_shift:row_shift + height, col_shift:col_shift + breadth].astype(jnp.float32)
        summed = summed + kernel[tap] * piece
    return summed

def tap_matrix(gain_pad, row_width, tap_block, block_len, half_reach):
    first_tap = (tap_block * block_len).astype(jnp.int32)
    segment = lax.dynamic_slice_in_dim(gain_pad, first_tap, block_len, 0)
    tap_ids = first_tap + jnp.arange(block_len, dtype=jnp.int32)
    keep = jnp.abs(tap_ids - half_reach) <= row_width
    segment = jnp.where(keep, segment, jnp.zeros_like(segment))
    padded = jnp.concatenate([segment, jnp.zeros((block_len + 1,), segment.dtype)])
    return jnp.tile(padded, block_len)[:2 * block_len * block_len].reshape(block_len, 2 * block_len)

def zonal_circle(circle, row_width, row_gains, first_block, block_count, active):
    circle_len = circle.shape[0]
    chans = circle.shape[1]
    block_len = circle_len // 8
    half_reach = circle_len // 4
    tap_blocks = 2 * half_reach // block_len + 1
    extended = jnp.concatenate([circle[circle_len - half_reach:], circle, circle[:half_reach + block_len]], axis=0)
    blocked = extended.reshape(-1, block_len, chans)
    gain_pad = jnp.concatenate([row_gains, jnp.zeros((tap_blocks * block_len - row_gains.shape[0],), row_gains.dtype)])
    row_width = row_width.astype(jnp.int32)
    if active:
        start_tap = ((half_reach - row_width) // block_len).astype(jnp.int32)
        stop_tap = ((half_reach + row_width) // block_len + 1).astype(jnp.int32)
    else:
        start_tap = jnp.zeros((), jnp.int32)
        stop_tap = jnp.full((), tap_blocks, jnp.int32)

    def add_block(tap_block, summed):
        matrix = tap_matrix(gain_pad, row_width, tap_block, block_len, half_reach)
        first_window = (first_block + tap_block).astype(jnp.int32)
        near = lax.dynamic_slice_in_dim(blocked, first_window, block_count, 0)
        after = lax.dynamic_slice_in_dim(blocked, first_window + 1, block_count, 0)
        window = jnp.concatenate([near, after], axis=1)
        return summed + jnp.einsum('ab,pbc->pac', matrix.astype(jnp.float32), window.astype(jnp.float32))
    return lax.fori_loop(start_tap, stop_tap, add_block, jnp.zeros((block_count, block_len, chans), jnp.float32))

def reference(inputs, metric, kernel_one, kernel_two, widths, zonal_gains, norm_gain, weight_in, weight_out):
    group = min(64, C)
    groups = C // group
    stacked = inputs.reshape(NLAT, NLON, groups, group).transpose(2, 0, 1, 3)
    kernels_one = kernel_one.reshape(9, groups, group).transpose(1, 0, 2)
    kernels_two = kernel_two.reshape(9, groups, group).transpose(1, 0, 2)

    def stencil_pair(operands):
        field, first_kernel, second_kernel = operands
        first = (field.astype(jnp.float32) * metric[:, :, None]).astype(jnp.bfloat16)
        stencil_one = stencil(extend_whole(first), first_kernel)
        second = (metric[:, :, None] * gelu_tanh(stencil_one)).astype(jnp.bfloat16)
        stencil_two = stencil(extend_whole(second), second_kernel)
        return (field.astype(jnp.float32) + stencil_two).astype(jnp.bfloat16)
    mixed = lax.map(stencil_pair, (stacked, kernels_one, kernels_two))
    mixed = mixed.transpose(1, 2, 0, 3).reshape(NLAT, NLON, C)

    def zonal_row(operands):
        circle, row_width, row_gains = operands
        filtered = zonal_circle(circle, row_width, row_gains, 0, 8, True)
        return filtered.reshape(NLON, C).astype(jnp.bfloat16)
    zonal = lax.map(zonal_row, (mixed, widths, zonal_gains))

    def row_group(operands):
        group_rows, group_zonal = operands
        flat = group_rows.reshape(-1, C).astype(jnp.float32)
        scale = lax.rsqrt(lax.optimization_barrier(jnp.mean(flat * flat, axis=1, keepdims=True)) + 1e-06)
        normed = (flat * scale * norm_gain).astype(jnp.bfloat16)
        hidden = gelu_tanh(jnp.dot(normed, weight_in, preferred_element_type=jnp.float32)).astype(jnp.bfloat16)
        pointwise = jnp.dot(hidden, weight_out, preferred_element_type=jnp.float32)
        combined = flat + group_zonal.reshape(-1, C).astype(jnp.float32) + pointwise
        return combined.astype(jnp.bfloat16).reshape(group_rows.shape)
    updated = lax.map(row_group, (mixed.reshape(NLAT // 8, 8, NLON, C), zonal.reshape(NLAT // 8, 8, NLON, C)))
    return updated.reshape(NLAT, NLON, C)
```

```python
import functools

import jax
import jax.numpy as jnp
from jax import lax
from jax.experimental import pallas as pl
from jax.experimental.pallas import tpu as pltpu
from jax.sharding import PartitionSpec as P

MESH = pl.DeviceIdType.MESH
LANES = 128
LEAD = 8


def round_up(value, step):
    return -(-value // step) * step


def gelu_tanh(values):
    return jax.nn.gelu(values, approximate=True)


def body(
    lats, n, rows, cols, chans, pad, reach,
    x_hbm, metric_ref, k1_ref, k2_ref, widths_ref, gains_ref, gain_ref, win_hbm, wout_hbm,
    out_hbm,
    x_ref, first, weights, held, sec, acc, mix, circ, zsend, zrecv, out_ref,
    edge, edge_in, strip, strip_in, corner_in, near,
    taps, lines, taps_one, win_ref, wout_ref,
    w_sem, o_sem,
    hs_sem, hr_sem, fs_sem, fr_sem, rs_sem, rr_sem,
):
    lat = lax.axis_index("lat")
    me = lax.axis_index("lon")
    chunks = rows // n
    half = n // 2
    wide = LEAD + pad
    slabs = 2 * reach + 1
    pitch = first.shape[1] // wide
    step = held.shape[1] // pad
    tiles = [slice(c * LANES, (c + 1) * LANES) for c in range(chans // LANES)]

    at_top = lat == 0
    at_bottom = lat == lats - 1
    up_lat = jnp.where(at_top, 0, lat - 1)
    up_lon = jnp.where(at_top, lax.rem(me + half, n), me)
    down_lat = jnp.where(at_bottom, lats - 1, lat + 1)
    down_lon = jnp.where(at_bottom, lax.rem(me + half, n), me)
    left = lax.rem(me + n - 1, n)
    right = lax.rem(me + 1, n)

    def before(lon):
        return lax.rem(lon + n - 1, n)

    def after(lon):
        return lax.rem(lon + 1, n)

    x_load = pltpu.make_async_copy(x_hbm, x_ref, w_sem.at[2])
    x_load.start()
    loads = [
        pltpu.make_async_copy(win_hbm, win_ref, w_sem.at[0]),
        pltpu.make_async_copy(wout_hbm, wout_ref, w_sem.at[1]),
    ]
    for load in loads:
        load.start()

    barrier = pltpu.get_barrier_semaphore()
    greeted = [
        (lat, left), (lat, right),
        (up_lat, up_lon), (up_lat, before(up_lon)), (up_lat, after(up_lon)),
        (down_lat, down_lon), (down_lat, before(down_lon)), (down_lat, after(down_lon)),
    ] + [(lat, lax.rem(me + o, n)) for o in range(1, n)]
    for device in greeted:
        pl.semaphore_signal(barrier, inc=1, device_id=device, device_id_type=MESH)

    halo = []

    def send_halo(src, dst, recv_index, device):
        copy = pltpu.make_async_remote_copy(
            src_ref=src, dst_ref=dst, send_sem=hs_sem.at[len(halo)], recv_sem=hr_sem.at[recv_index],
            device_id=device, device_id_type=MESH,
        )
        copy.start()
        halo.append(copy)

    def recv_halo(src, dst, recv_index):
        pltpu.make_async_remote_copy(
            src_ref=src, dst_ref=dst, send_sem=hs_sem.at[0], recv_sem=hr_sem.at[recv_index],
            device_id=(lat, right), device_id_type=MESH,
        ).wait_recv()

    def spread(block, c):
        return jnp.broadcast_to(block[:, c:c + 1], (rows, LANES))

    def enter(c):
        weight = spread(metric_ref, c)
        at = (LEAD + c) * pitch + 2
        weights[at:at + rows] = weight
        for t, lanes in enumerate(tiles):
            cells = x_ref[c, :, lanes].astype(jnp.float32)
            held[t, c * step:c * step + rows] = cells
            value = (cells * weight).astype(jnp.bfloat16)
            first[t, at:at + rows] = value.astype(jnp.float32)
            if c < 2:
                strip[0, c, :, lanes] = value
            if c >= cols - 2:
                strip[1, c - cols + 2, :, lanes] = value

    rims = [0, 1, cols - 2, cols - 1]
    x_load.wait()
    for c in rims:
        enter(c)
    pl.semaphore_wait(barrier, len(greeted))

    up_side = jnp.where(at_top, 0, 1)
    down_side = jnp.where(at_bottom, 1, 0)
    for s, device in ((0, left), (1, right)):
        send_halo(strip.at[s], strip_in.at[1 - s], 4 + s, (lat, device))
        send_halo(metric_ref, near.at[1 - s], 10 + s, (lat, device))
    for side, src, device_lat, device_lon in (
        (up_side, 0, up_lat, up_lon), (down_side, rows - 8, down_lat, down_lon)
    ):
        send_halo(metric_ref, near.at[2 + side], 12 + side, (device_lat, device_lon))
        for s, lon in ((0, before(device_lon)), (1, after(device_lon))):
            send_halo(
                strip.at[s, :, pl.ds(src, 8)], corner_in.at[side, 1 - s], 6 + 2 * side + s, (device_lat, lon)
            )
            send_halo(metric_ref, near.at[4 + 2 * side + 1 - s], 14 + 2 * side + s, (device_lat, lon))

    for c in range(2, cols - 2):
        enter(c)
    for slot, row in enumerate((0, 1, rows - 2, rows - 1)):
        for t, lanes in enumerate(tiles):
            line = first[t, pl.ds(LEAD * pitch + row + 2, pad, stride=pitch), :]
            edge[slot, :, lanes] = line.astype(jnp.bfloat16)
    for i in range(2):
        up_slot = jnp.where(at_top, 1 - i, 2 + i)
        down_slot = jnp.where(at_bottom, 3 - i, i)
        send_halo(edge.at[i], edge_in.at[up_slot], up_slot, (up_lat, up_lon))
        send_halo(edge.at[2 + i], edge_in.at[down_slot], down_slot, (down_lat, down_lon))

    tap_lanes = taps.shape[2]
    lane_ids = lax.broadcasted_iota(jnp.int32, (pad, tap_lanes), 1)
    taps_one[0, 0:9] = k1_ref[...]
    for a in range(3):
        taps_one[1, 3 * a:3 * a + 3] = k1_ref[6 - 3 * a:9 - 3 * a, :]
    count = gains_ref.shape[1]
    center = (count - 1) // 2
    lines[...] = jnp.zeros(lines.shape, jnp.float32)
    lines[:, 0:count] = gains_ref[...].astype(jnp.float32)
    for k in range(chunks):
        line = jnp.broadcast_to(lines[pl.ds(k * n + me, 1), :], (pad, tap_lanes))
        kept = jnp.abs(lane_ids - center) <= widths_ref[k * n + me]
        line = jnp.where(kept, line, 0.0)
        shifted = pltpu.roll(line, 0, 1, stride=1, stride_axis=0)
        total = jnp.zeros((pad, tap_lanes), jnp.float32)
        for d in range(slabs):
            moved = pltpu.roll(shifted, (pad - cols) * d, 1) if d else shifted
            inside = (lane_ids >= pad * d) & (lane_ids < pad * d + cols)
            total = jnp.where(inside, moved, total)
        taps[k] = total.astype(jnp.bfloat16)

    for s in range(2):
        recv_halo(strip.at[s], strip_in.at[1 - s], 4 + s)
        recv_halo(metric_ref, near.at[1 - s], 10 + s)
    for s, start, c, from_col in ((0, LEAD - 2, LEAD - 1, cols - 1), (1, LEAD + cols, LEAD + cols, 0)):
        weights[c * pitch + 2:c * pitch + 2 + rows] = spread(near.at[s], from_col)
        for j in range(2):
            at = (start + j) * pitch + 2
            for t, lanes in enumerate(tiles):
                first[t, at:at + rows] = strip_in[s, j, :, lanes].astype(jnp.float32)

    def join_rows():
        for slot in range(4):
            recv_halo(edge.at[0], edge_in.at[slot], slot)
        for side in range(2):
            recv_halo(metric_ref, near.at[2 + side], 12 + side)
            for s in range(2):
                recv_halo(strip.at[s, :, pl.ds(0, 8)], corner_in.at[side, 1 - s], 6 + 2 * side + s)
                recv_halo(metric_ref, near.at[4 + 2 * side + 1 - s], 14 + 2 * side + s)
        diagonal = lax.broadcasted_iota(jnp.int32, (pad, cols), 0) == lax.broadcasted_iota(
            jnp.int32, (pad, cols), 1
        )
        for slot in range(4):
            row = slot if slot < 2 else rows + slot
            for t, lanes in enumerate(tiles):
                line = edge_in[slot, :, lanes].astype(jnp.float32)
                first[t, pl.ds(LEAD * pitch + row, cols, stride=pitch), :] = line[0:cols]
        for side, pole in ((0, at_top), (1, at_bottom)):
            lower = (rows - 1, 0)[side]
            source = jnp.where(pole, rows - 1 - lower, lower)
            row = (1, rows + 2)[side]
            line = jnp.broadcast_to(near[2 + side, pl.ds(source, 1), :], (pad, cols))
            column = jnp.sum(jnp.where(diagonal, line, 0.0), axis=1, keepdims=True)
            column = jnp.broadcast_to(column, (pad, LANES))
            weights[pl.ds(LEAD * pitch + row, cols, stride=pitch), :] = column[0:cols]
            for s, c, from_col in ((0, LEAD - 1, cols - 1), (1, LEAD + cols, 0)):
                cell = near[4 + 2 * side + s, pl.ds(source, 1), :]
                weights[c * pitch + row:c * pitch + row + 1] = jnp.broadcast_to(
                    cell[:, from_col:from_col + 1], (1, LANES)
                )
            top = (0, rows + 2)[side]
            for s, start in ((0, LEAD - 2), (1, LEAD + cols)):
                for j in range(2):
                    at = (start + j) * pitch + top
                    for t, lanes in enumerate(tiles):
                        cells = corner_in[side, s, j, :, lanes].astype(jnp.float32)
                        if side == 0:
                            plain, one, two = cells[6:8], cells[1:2], cells[0:1]
                        else:
                            plain, one, two = cells[0:2], cells[7:8], cells[6:7]
                        first[t, at:at + 1] = jnp.where(pole, one, plain[0:1])
                        first[t, at + 1:at + 2] = jnp.where(pole, two, plain[1:2])

    def stencil(load, kernel):
        sums = [None, None, None]
        for a in range(3):
            line = load(a)
            for b in range(3):
                term = kernel(a, b) * line
                sums[b] = term if sums[b] is None else sums[b] + term
        return pltpu.roll(sums[0], 1, 0) + sums[1] + pltpu.roll(sums[2], wide - 1, 0)

    def second_row(p, carry):
        flip = ((p == 0) & at_top) | ((p == rows + 1) & at_bottom)
        which = jnp.where(flip, 1, 0)
        weight = weights[pl.ds(p + 1, wide, stride=pitch), :]
        for t, lanes in enumerate(tiles):
            value = stencil(
                lambda a: first[t, pl.ds(p + a, wide, stride=pitch), :],
                lambda a, b: taps_one[which, 3 * a + b:3 * a + b + 1, lanes],
            )
            value = weight * gelu_tanh(value)
            sec[p, :, lanes] = value.astype(jnp.bfloat16).astype(jnp.float32)
        return carry

    col_ids = lax.broadcasted_iota(jnp.int32, (pad, LANES), 0)

    def mixed_row(i, carry):
        for t, lanes in enumerate(tiles):
            value = stencil(
                lambda a: sec[i + a, :, lanes],
                lambda a, b: k2_ref[3 * a + b:3 * a + b + 1, lanes],
            )
            value = held[t, pl.ds(i, pad, stride=step), :] + value[LEAD:, :]
            mix[i, :, lanes] = jnp.where(col_ids < cols, value, 0.0).astype(jnp.bfloat16)
        return carry

    forward = []
    order = list(range(1, chunks - 1)) + [0] + ([chunks - 1] if chunks > 1 else [])
    done = set()
    joined = False
    for k in order:
        if not joined and k in (0, chunks - 1):
            join_rows()
            joined = True
        needed = [p for p in range(k * n, (k + 1) * n + 2) if p not in done]
        done.update(needed)
        lax.fori_loop(needed[0], needed[-1] + 1, second_row, 0)
        lax.fori_loop(k * n, (k + 1) * n, mixed_row, 0)
        for o in range(1, n):
            target = lax.rem(me + o, n)
            copy = pltpu.make_async_remote_copy(
                src_ref=mix.at[k * n + target], dst_ref=circ.at[k, me + reach],
                send_sem=fs_sem.at[k, o], recv_sem=fr_sem.at[k, o],
                device_id=(lat, target), device_id_type=MESH,
            )
            copy.start()
            forward.append(copy)
        circ[k, me + reach] = mix[k * n + me]

    for copy in halo:
        copy.wait_send()
    for load in loads:
        load.wait()

    group = 8

    def network(g, carry):
        flat = mix[pl.ds(g * group, group)].reshape(group * pad, chans).astype(jnp.float32)
        scale = lax.rsqrt(jnp.mean(flat * flat, axis=1, keepdims=True) + 1e-06)
        normed = (flat * scale * gain_ref[...]).astype(jnp.bfloat16)
        hidden = gelu_tanh(
            jnp.dot(normed, win_ref[...], preferred_element_type=jnp.float32)
        ).astype(jnp.bfloat16)
        point = jnp.dot(hidden, wout_ref[...], preferred_element_type=jnp.float32)
        acc[pl.ds(g * group, group)] = (flat + point).reshape(group, pad, chans)
        return carry

    lax.fori_loop(0, rows // group, network, 0)

    back = []
    for k in order:
        for o in range(1, n):
            source = lax.rem(me + n - o, n)
            pltpu.make_async_remote_copy(
                src_ref=mix.at[k * n], dst_ref=circ.at[k, source + reach],
                send_sem=fs_sem.at[k, o], recv_sem=fr_sem.at[k, o],
                device_id=(lat, source), device_id_type=MESH,
            ).wait_recv()
        for e in range(reach):
            circ[k, e] = circ[k, n + e]
            circ[k, n + reach + e] = circ[k, reach + e]

        def filter_block(a, carry):
            window = circ[k, pl.ds(a, slabs)].reshape(slabs * pad, chans)
            result = jnp.dot(
                taps[k, :, 0:slabs * pad], window, preferred_element_type=jnp.float32
            )
            zsend[k * n + a] = result.astype(jnp.bfloat16)
            return carry

        lax.fori_loop(0, n, filter_block, 0, unroll=4)
        for o in range(1, n):
            target = lax.rem(me + o, n)
            copy = pltpu.make_async_remote_copy(
                src_ref=zsend.at[k * n + target], dst_ref=zrecv.at[k * n + me],
                send_sem=rs_sem.at[k, o], recv_sem=rr_sem.at[k, o],
                device_id=(lat, target), device_id_type=MESH,
            )
            copy.start()
            back.append(copy)
        zrecv[k * n + me] = zsend[k * n + me]

    stores = []
    for k in order:
        for o in range(1, n):
            source = lax.rem(me + n - o, n)
            pltpu.make_async_remote_copy(
                src_ref=zsend.at[k * n], dst_ref=zrecv.at[k * n + source],
                send_sem=rs_sem.at[k, o], recv_sem=rr_sem.at[k, o],
                device_id=(lat, source), device_id_type=MESH,
            ).wait_recv()

        def finish(i, carry):
            for t, lanes in enumerate(tiles):
                value = acc[i, :, lanes] + zrecv[i, :, lanes].astype(jnp.float32)
                held[t, pl.ds(i, cols, stride=step), :] = value[0:cols]
            return carry

        lax.fori_loop(k * n, (k + 1) * n, finish, 0)
        for c in range(cols):
            for t, lanes in enumerate(tiles):
                at = c * step + k * n
                out_ref[c, k * n:(k + 1) * n, lanes] = held[t, at:at + n].astype(jnp.bfloat16)
        store = pltpu.make_async_copy(
            out_ref.at[:, pl.ds(k * n, n)], out_hbm.at[:, pl.ds(k * n, n)], o_sem.at[k]
        )
        store.start()
        stores.append(store)

    for copy in forward + back:
        copy.wait_send()
    for store in stores:
        store.wait()


def local(
    lats, n,
    inputs, metric, kernel_one, kernel_two, widths, zonal_gains, norm_gain, weight_in, weight_out
):
    rows, cols, chans = inputs.shape
    pad = round_up(cols, 16)
    wide = LEAD + pad
    reach = n // 4
    slabs = 2 * reach + 1
    count = zonal_gains.shape[1]
    tap_lanes = round_up(max(slabs * pad, count + pad - 1), LANES)
    pitch = (rows + 4) | 1
    step = rows | 1

    chunks = rows // n
    tiles = chans // LANES
    vmem = pl.BlockSpec(memory_space=pltpu.VMEM)
    hbm = pl.BlockSpec(memory_space=pl.ANY)
    sem = pltpu.SemaphoreType.DMA
    out = pl.pallas_call(
        functools.partial(body, lats, n, rows, cols, chans, pad, reach),
        out_shape=jax.ShapeDtypeStruct((cols, rows, chans), jnp.bfloat16),
        in_specs=[hbm] + [vmem] * 3
        + [pl.BlockSpec(memory_space=pltpu.SMEM), vmem, vmem]
        + [hbm] * 2,
        out_specs=hbm,
        scratch_shapes=[
            pltpu.VMEM((cols, rows, chans), jnp.bfloat16),
            pltpu.VMEM((tiles, wide * pitch, LANES), jnp.float32),
            pltpu.VMEM((wide * pitch, LANES), jnp.float32),
            pltpu.VMEM((tiles, pad * step, LANES), jnp.float32),
            pltpu.VMEM((rows + 2, wide, chans), jnp.float32),
            pltpu.VMEM((rows, pad, chans), jnp.float32),
            pltpu.VMEM((rows, pad, chans), jnp.bfloat16),
            pltpu.VMEM((chunks, n + 2 * reach, pad, chans), jnp.bfloat16),
            pltpu.VMEM((rows, pad, chans), jnp.bfloat16),
            pltpu.VMEM((rows, pad, chans), jnp.bfloat16),
            pltpu.VMEM((cols, rows, chans), jnp.bfloat16),
            pltpu.VMEM((4, pad, chans), jnp.bfloat16),
            pltpu.VMEM((4, pad, chans), jnp.bfloat16),
            pltpu.VMEM((2, 2, rows, chans), jnp.bfloat16),
            pltpu.VMEM((2, 2, rows, chans), jnp.bfloat16),
            pltpu.VMEM((2, 2, 2, 8, chans), jnp.bfloat16),
            pltpu.VMEM((8, rows, cols), jnp.float32),
            pltpu.VMEM((chunks, pad, tap_lanes), jnp.bfloat16),
            pltpu.VMEM((rows, tap_lanes), jnp.float32),
            pltpu.VMEM((2, 16, chans), jnp.float32),
            pltpu.VMEM(weight_in.shape, jnp.bfloat16),
            pltpu.VMEM(weight_out.shape, jnp.bfloat16),
            sem((3,)), sem((chunks,)),
            sem((18,)), sem((18,)),
            sem((chunks, n)), sem((chunks, n)), sem((chunks, n)), sem((chunks, n)),
        ],
        compiler_params=pltpu.CompilerParams(
            collective_id=0, has_side_effects=True, vmem_limit_bytes=60 * 2**20
        ),
    )(
        inputs.transpose(1, 0, 2), metric, kernel_one, kernel_two, widths, zonal_gains, norm_gain.reshape(1, chans),
        weight_in, weight_out,
    )
    return out.transpose(1, 0, 2)


def solution(mesh):
    placed = (
        P("lat", "lon", None),
        P("lat", "lon"),
        P(),
        P(),
        P("lat"),
        P("lat", None),
        P(),
        P(),
        P(),
    )
    return jax.shard_map(
        functools.partial(local, mesh.shape["lat"], mesh.shape["lon"]),
        mesh=mesh, in_specs=placed, out_specs=P("lat", "lon", None), check_vma=False,
    )
```

```python
import functools

import jax
import jax.numpy as jnp
from jax import lax
from jax.experimental import pallas as pl
from jax.experimental.pallas import tpu as pltpu
from jax.sharding import PartitionSpec as P

MESH = pl.DeviceIdType.MESH
LANES = 128
LEAD = 8


def round_up(value, step):
    return -(-value // step) * step


def gelu_tanh(values):
    return jax.nn.gelu(values, approximate=True)


def body(
    lats, n, rows, cols, chans, pad, reach,
    x_hbm, metric_ref, k1_ref, k2_ref, widths_ref, gains_ref, gain_ref, win_hbm, wout_hbm,
    out_hbm,
    x_ref, first, weights, held, sec, acc, mix, circ, zsend, zrecv, out_ref,
    edge, edge_in, strip, strip_in, corner_in, near,
    taps, lines, taps_one, win_ref, wout_ref,
    w_sem, o_sem,
    hs_sem, hr_sem, fs_sem, fr_sem, rs_sem, rr_sem,
):
    lat = lax.axis_index("lat")
    me = lax.axis_index("lon")
    chunks = rows // n
    half = n // 2
    wide = LEAD + pad
    slabs = 2 * reach + 1
    pitch = first.shape[1] // wide
    step = held.shape[1] // pad
    tiles = [slice(c * LANES, (c + 1) * LANES) for c in range(chans // LANES)]

    at_top = lat == 0
    at_bottom = lat == lats - 1
    up_lat = jnp.where(at_top, 0, lat - 1)
    up_lon = jnp.where(at_top, lax.rem(me + half, n), me)
    down_lat = jnp.where(at_bottom, lats - 1, lat + 1)
    down_lon = jnp.where(at_bottom, lax.rem(me + half, n), me)
    left = lax.rem(me + n - 1, n)
    right = lax.rem(me + 1, n)

    def before(lon):
        return lax.rem(lon + n - 1, n)

    def after(lon):
        return lax.rem(lon + 1, n)

    x_load = pltpu.make_async_copy(x_hbm, x_ref, w_sem.at[2])
    x_load.start()
    loads = [
        pltpu.make_async_copy(win_hbm, win_ref, w_sem.at[0]),
        pltpu.make_async_copy(wout_hbm, wout_ref, w_sem.at[1]),
    ]
    for load in loads:
        load.start()

    barrier = pltpu.get_barrier_semaphore()
    greeted = [
        (lat, left), (lat, right),
        (up_lat, up_lon), (up_lat, before(up_lon)), (up_lat, after(up_lon)),
        (down_lat, down_lon), (down_lat, before(down_lon)), (down_lat, after(down_lon)),
    ] + [(lat, lax.rem(me + o, n)) for o in range(1, n)]
    for device in greeted:
        pl.semaphore_signal(barrier, inc=1, device_id=device, device_id_type=MESH)

    halo = []

    def send_halo(src, dst, recv_index, device):
        copy = pltpu.make_async_remote_copy(
            src_ref=src, dst_ref=dst, send_sem=hs_sem.at[len(halo)], recv_sem=hr_sem.at[recv_index],
            device_id=device, device_id_type=MESH,
        )
        copy.start()
        halo.append(copy)

    def recv_halo(src, dst, recv_index):
        pltpu.make_async_remote_copy(
            src_ref=src, dst_ref=dst, send_sem=hs_sem.at[0], recv_sem=hr_sem.at[recv_index],
            device_id=(lat, right), device_id_type=MESH,
        ).wait_recv()

    def spread(block, c):
        return jnp.broadcast_to(block[:, c:c + 1], (rows, LANES))

    def enter(c):
        weight = spread(metric_ref, c)
        at = (LEAD + c) * pitch + 2
        weights[at:at + rows] = weight
        for t, lanes in enumerate(tiles):
            cells = x_ref[c, :, lanes].astype(jnp.float32)
            held[t, c * step:c * step + rows] = cells
            value = (cells * weight).astype(jnp.bfloat16)
            first[t, at:at + rows] = value.astype(jnp.float32)
            if c < 2:
                strip[0, c, :, lanes] = value
            if c >= cols - 2:
                strip[1, c - cols + 2, :, lanes] = value

    rims = [0, 1, cols - 2, cols - 1]
    x_load.wait()
    for c in rims:
        enter(c)
    pl.semaphore_wait(barrier, len(greeted))

    up_side = jnp.where(at_top, 0, 1)
    down_side = jnp.where(at_bottom, 1, 0)
    for s, device in ((0, left), (1, right)):
        send_halo(strip.at[s], strip_in.at[1 - s], 4 + s, (lat, device))
        send_halo(metric_ref, near.at[1 - s], 10 + s, (lat, device))
    for side, src, device_lat, device_lon in (
        (up_side, 0, up_lat, up_lon), (down_side, rows - 8, down_lat, down_lon)
    ):
        send_halo(metric_ref, near.at[2 + side], 12 + side, (device_lat, device_lon))
        for s, lon in ((0, before(device_lon)), (1, after(device_lon))):
            send_halo(
                strip.at[s, :, pl.ds(src, 8)], corner_in.at[side, 1 - s], 6 + 2 * side + s, (device_lat, lon)
            )
            send_halo(metric_ref, near.at[4 + 2 * side + 1 - s], 14 + 2 * side + s, (device_lat, lon))

    for c in range(2, cols - 2):
        enter(c)
    for slot, row in enumerate((0, 1, rows - 2, rows - 1)):
        for t, lanes in enumerate(tiles):
            line = first[t, pl.ds(LEAD * pitch + row + 2, pad, stride=pitch), :]
            edge[slot, :, lanes] = line.astype(jnp.bfloat16)
    for i in range(2):
        up_slot = jnp.where(at_top, 1 - i, 2 + i)
        down_slot = jnp.where(at_bottom, 3 - i, i)
        send_halo(edge.at[i], edge_in.at[up_slot], up_slot, (up_lat, up_lon))
        send_halo(edge.at[2 + i], edge_in.at[down_slot], down_slot, (down_lat, down_lon))

    tap_lanes = taps.shape[2]
    lane_ids = lax.broadcasted_iota(jnp.int32, (pad, tap_lanes), 1)
    taps_one[0, 0:9] = k1_ref[...]
    for a in range(3):
        taps_one[1, 3 * a:3 * a + 3] = k1_ref[6 - 3 * a:9 - 3 * a, :]
    count = gains_ref.shape[1]
    center = (count - 1) // 2
    lines[...] = jnp.zeros(lines.shape, jnp.float32)
    lines[:, 0:count] = gains_ref[...].astype(jnp.float32)
    for k in range(chunks):
        line = jnp.broadcast_to(lines[pl.ds(k * n + me, 1), :], (pad, tap_lanes))
        kept = jnp.abs(lane_ids - center) <= widths_ref[k * n + me]
        line = jnp.where(kept, line, 0.0)
        shifted = pltpu.roll(line, 0, 1, stride=1, stride_axis=0)
        total = jnp.zeros((pad, tap_lanes), jnp.float32)
        for d in range(slabs):
            moved = pltpu.roll(shifted, (pad - cols) * d, 1) if d else shifted
            inside = (lane_ids >= pad * d) & (lane_ids < pad * d + cols)
            total = jnp.where(inside, moved, total)
        taps[k] = total.astype(jnp.bfloat16)

    for s in range(2):
        recv_halo(strip.at[s], strip_in.at[1 - s], 4 + s)
        recv_halo(metric_ref, near.at[1 - s], 10 + s)
    for s, start, c, from_col in ((0, LEAD - 2, LEAD - 1, cols - 1), (1, LEAD + cols, LEAD + cols, 0)):
        weights[c * pitch + 2:c * pitch + 2 + rows] = spread(near.at[s], from_col)
        for j in range(2):
            at = (start + j) * pitch + 2
            for t, lanes in enumerate(tiles):
                first[t, at:at + rows] = strip_in[s, j, :, lanes].astype(jnp.float32)

    def join_rows():
        for slot in range(4):
            recv_halo(edge.at[0], edge_in.at[slot], slot)
        for side in range(2):
            recv_halo(metric_ref, near.at[2 + side], 12 + side)
            for s in range(2):
                recv_halo(strip.at[s, :, pl.ds(0, 8)], corner_in.at[side, 1 - s], 6 + 2 * side + s)
                recv_halo(metric_ref, near.at[4 + 2 * side + 1 - s], 14 + 2 * side + s)
        diagonal = lax.broadcasted_iota(jnp.int32, (pad, cols), 0) == lax.broadcasted_iota(
            jnp.int32, (pad, cols), 1
        )
        for slot in range(4):
            row = slot if slot < 2 else rows + slot
            for t, lanes in enumerate(tiles):
                line = edge_in[slot, :, lanes].astype(jnp.float32)
                first[t, pl.ds(LEAD * pitch + row, cols, stride=pitch), :] = line[0:cols]
        for side, pole in ((0, at_top), (1, at_bottom)):
            lower = (rows - 1, 0)[side]
            source = jnp.where(pole, rows - 1 - lower, lower)
            row = (1, rows + 2)[side]
            line = jnp.broadcast_to(near[2 + side, pl.ds(source, 1), :], (pad, cols))
            column = jnp.sum(jnp.where(diagonal, line, 0.0), axis=1, keepdims=True)
            column = jnp.broadcast_to(column, (pad, LANES))
            weights[pl.ds(LEAD * pitch + row, cols, stride=pitch), :] = column[0:cols]
            for s, c, from_col in ((0, LEAD - 1, cols - 1), (1, LEAD + cols, 0)):
                cell = near[4 + 2 * side + s, pl.ds(source, 1), :]
                weights[c * pitch + row:c * pitch + row + 1] = jnp.broadcast_to(
                    cell[:, from_col:from_col + 1], (1, LANES)
                )
            top = (0, rows + 2)[side]
            for s, start in ((0, LEAD - 2), (1, LEAD + cols)):
                for j in range(2):
                    at = (start + j) * pitch + top
                    for t, lanes in enumerate(tiles):
                        cells = corner_in[side, s, j, :, lanes].astype(jnp.float32)
                        if side == 0:
                            plain, one, two = cells[6:8], cells[1:2], cells[0:1]
                        else:
                            plain, one, two = cells[0:2], cells[7:8], cells[6:7]
                        first[t, at:at + 1] = jnp.where(pole, one, plain[0:1])
                        first[t, at + 1:at + 2] = jnp.where(pole, two, plain[1:2])

    def stencil(load, kernel):
        sums = [None, None, None]
        for a in range(3):
            line = load(a)
            for b in range(3):
                term = kernel(a, b) * line
                sums[b] = term if sums[b] is None else sums[b] + term
        return pltpu.roll(sums[0], 1, 0) + sums[1] + pltpu.roll(sums[2], wide - 1, 0)

    def second_row(p, carry):
        flip = ((p == 0) & at_top) | ((p == rows + 1) & at_bottom)
        which = jnp.where(flip, 1, 0)
        weight = weights[pl.ds(p + 1, wide, stride=pitch), :]
        for t, lanes in enumerate(tiles):
            value = stencil(
                lambda a: first[t, pl.ds(p + a, wide, stride=pitch), :],
                lambda a, b: taps_one[which, 3 * a + b:3 * a + b + 1, lanes],
            )
            value = weight * gelu_tanh(value)
            sec[p, :, lanes] = value.astype(jnp.bfloat16).astype(jnp.float32)
        return carry

    col_ids = lax.broadcasted_iota(jnp.int32, (pad, LANES), 0)

    def mixed_row(i, carry):
        for t, lanes in enumerate(tiles):
            value = stencil(
                lambda a: sec[i + a, :, lanes],
                lambda a, b: k2_ref[3 * a + b:3 * a + b + 1, lanes],
            )
            value = held[t, pl.ds(i, pad, stride=step), :] + value[LEAD:, :]
            mix[i, :, lanes] = jnp.where(col_ids < cols, value, 0.0).astype(jnp.bfloat16)
        return carry

    forward = []
    order = list(range(1, chunks - 1)) + [0] + ([chunks - 1] if chunks > 1 else [])
    done = set()
    joined = False
    for k in order:
        if not joined and k in (0, chunks - 1):
            join_rows()
            joined = True
        needed = [p for p in range(k * n, (k + 1) * n + 2) if p not in done]
        done.update(needed)
        lax.fori_loop(needed[0], needed[-1] + 1, second_row, 0)
        lax.fori_loop(k * n, (k + 1) * n, mixed_row, 0)
        for o in range(1, n):
            target = lax.rem(me + o, n)
            copy = pltpu.make_async_remote_copy(
                src_ref=mix.at[k * n + target], dst_ref=circ.at[k, me + reach],
                send_sem=fs_sem.at[k, o], recv_sem=fr_sem.at[k, o],
                device_id=(lat, target), device_id_type=MESH,
            )
            copy.start()
            forward.append(copy)
        circ[k, me + reach] = mix[k * n + me]

    for copy in halo:
        copy.wait_send()
    for load in loads:
        load.wait()

    group = 8

    def network(g, carry):
        flat = mix[pl.ds(g * group, group)].reshape(group * pad, chans).astype(jnp.float32)
        scale = lax.rsqrt(jnp.mean(flat * flat, axis=1, keepdims=True) + 1e-06)
        normed = (flat * scale * gain_ref[...]).astype(jnp.bfloat16)
        hidden = gelu_tanh(
            jnp.dot(normed, win_ref[...], preferred_element_type=jnp.float32)
        ).astype(jnp.bfloat16)
        point = jnp.dot(hidden, wout_ref[...], preferred_element_type=jnp.float32)
        acc[pl.ds(g * group, group)] = (flat + point).reshape(group, pad, chans)
        return carry

    lax.fori_loop(0, rows // group, network, 0)

    back = []
    for k in order:
        for o in range(1, n):
            source = lax.rem(me + n - o, n)
            pltpu.make_async_remote_copy(
                src_ref=mix.at[k * n], dst_ref=circ.at[k, source + reach],
                send_sem=fs_sem.at[k, o], recv_sem=fr_sem.at[k, o],
                device_id=(lat, source), device_id_type=MESH,
            ).wait_recv()
        for e in range(reach):
            circ[k, e] = circ[k, n + e]
            circ[k, n + reach + e] = circ[k, reach + e]

        def filter_block(a, carry):
            window = circ[k, pl.ds(a, slabs)].reshape(slabs * pad, chans)
            result = jnp.dot(
                taps[k, :, 0:slabs * pad], window, preferred_element_type=jnp.float32
            )
            zsend[a * chunks + k] = result.astype(jnp.bfloat16)
            return carry

        lax.fori_loop(0, n, filter_block, 0, unroll=4)
        for o in range(1, n):
            target = lax.rem(me + o, n)
            copy = pltpu.make_async_remote_copy(
                src_ref=zsend.at[target * chunks + k], dst_ref=zrecv.at[me * chunks + k],
                send_sem=rs_sem.at[k, o], recv_sem=rr_sem.at[k, o],
                device_id=(lat, target), device_id_type=MESH,
            )
            copy.start()
            back.append(copy)
        zrecv[me * chunks + k] = zsend[me * chunks + k]

    stores = []
    for k in order:
        for o in range(1, n):
            source = lax.rem(me + n - o, n)
            pltpu.make_async_remote_copy(
                src_ref=zsend.at[k], dst_ref=zrecv.at[source * chunks + k],
                send_sem=rs_sem.at[k, o], recv_sem=rr_sem.at[k, o],
                device_id=(lat, source), device_id_type=MESH,
            ).wait_recv()

        def finish(i, carry):
            for t, lanes in enumerate(tiles):
                value = acc[i, :, lanes] + zrecv[(i - k * n) * chunks + k, :, lanes].astype(jnp.float32)
                held[t, pl.ds(i, cols, stride=step), :] = value[0:cols]
            return carry

        lax.fori_loop(k * n, (k + 1) * n, finish, 0)
        for c in range(cols):
            for t, lanes in enumerate(tiles):
                at = c * step + k * n
                out_ref[c, k * n:(k + 1) * n, lanes] = held[t, at:at + n].astype(jnp.bfloat16)
        store = pltpu.make_async_copy(
            out_ref.at[:, pl.ds(k * n, n)], out_hbm.at[:, pl.ds(k * n, n)], o_sem.at[k]
        )
        store.start()
        stores.append(store)

    for copy in forward + back:
        copy.wait_send()
    for store in stores:
        store.wait()


def local(
    lats, n,
    inputs, metric, kernel_one, kernel_two, widths, zonal_gains, norm_gain, weight_in, weight_out
):
    rows, cols, chans = inputs.shape
    pad = round_up(cols, 16)
    wide = LEAD + pad
    reach = n // 4
    slabs = 2 * reach + 1
    count = zonal_gains.shape[1]
    tap_lanes = round_up(max(slabs * pad, count + pad - 1), LANES)
    pitch = (rows + 4) | 1
    step = rows | 1

    chunks = rows // n
    tiles = chans // LANES
    vmem = pl.BlockSpec(memory_space=pltpu.VMEM)
    hbm = pl.BlockSpec(memory_space=pl.ANY)
    sem = pltpu.SemaphoreType.DMA
    out = pl.pallas_call(
        functools.partial(body, lats, n, rows, cols, chans, pad, reach),
        out_shape=jax.ShapeDtypeStruct((cols, rows, chans), jnp.bfloat16),
        in_specs=[hbm] + [vmem] * 3
        + [pl.BlockSpec(memory_space=pltpu.SMEM), vmem, vmem]
        + [hbm] * 2,
        out_specs=hbm,
        scratch_shapes=[
            pltpu.VMEM((cols, rows, chans), jnp.bfloat16),
            pltpu.VMEM((tiles, wide * pitch, LANES), jnp.float32),
            pltpu.VMEM((wide * pitch, LANES), jnp.float32),
            pltpu.VMEM((tiles, pad * step, LANES), jnp.float32),
            pltpu.VMEM((rows + 2, wide, chans), jnp.float32),
            pltpu.VMEM((rows, pad, chans), jnp.float32),
            pltpu.VMEM((rows, pad, chans), jnp.bfloat16),
            pltpu.VMEM((chunks, n + 2 * reach, pad, chans), jnp.bfloat16),
            pltpu.VMEM((rows, pad, chans), jnp.bfloat16),
            pltpu.VMEM((rows, pad, chans), jnp.bfloat16),
            pltpu.VMEM((cols, rows, chans), jnp.bfloat16),
            pltpu.VMEM((4, pad, chans), jnp.bfloat16),
            pltpu.VMEM((4, pad, chans), jnp.bfloat16),
            pltpu.VMEM((2, 2, rows, chans), jnp.bfloat16),
            pltpu.VMEM((2, 2, rows, chans), jnp.bfloat16),
            pltpu.VMEM((2, 2, 2, 8, chans), jnp.bfloat16),
            pltpu.VMEM((8, rows, cols), jnp.float32),
            pltpu.VMEM((chunks, pad, tap_lanes), jnp.bfloat16),
            pltpu.VMEM((rows, tap_lanes), jnp.float32),
            pltpu.VMEM((2, 16, chans), jnp.float32),
            pltpu.VMEM(weight_in.shape, jnp.bfloat16),
            pltpu.VMEM(weight_out.shape, jnp.bfloat16),
            sem((3,)), sem((chunks,)),
            sem((18,)), sem((18,)),
            sem((chunks, n)), sem((chunks, n)), sem((chunks, n)), sem((chunks, n)),
        ],
        compiler_params=pltpu.CompilerParams(
            collective_id=0, has_side_effects=True, vmem_limit_bytes=60 * 2**20
        ),
    )(
        inputs.transpose(1, 0, 2), metric, kernel_one, kernel_two, widths, zonal_gains, norm_gain.reshape(1, chans),
        weight_in, weight_out,
    )
    return out.transpose(1, 0, 2)


def solution(mesh):
    placed = (
        P("lat", "lon", None),
        P("lat", "lon"),
        P(),
        P(),
        P("lat"),
        P("lat", None),
        P(),
        P(),
        P(),
    )
    return jax.shard_map(
        functools.partial(local, mesh.shape["lat"], mesh.shape["lon"]),
        mesh=mesh, in_specs=placed, out_specs=P("lat", "lon", None), check_vma=False,
    )
```
